32 devices in a mesh: section: 8 (over z, x), tensor: 4 (over y, core).
Axes of the slice: x: 2, y: 2, z: 4, core: 2. Of those that a mesh axis runs over, the one named last changes fastest.
Arguments:
- layer_input: bfloat16 [3072, 5120], P('section', 'tensor'), may hold values from -6 to 6
- query_rows: bfloat16 [3072, 4096], P('section', 'tensor'), may hold values from -4.6 to 4.6
- key_rows: bfloat16 [3072, 4096], P('section', 'tensor'), may hold values from -4.6 to 4.6
- value_rows: bfloat16 [3072, 4096], P('section', 'tensor'), may hold values from -6 to 6
- out_grad: bfloat16 [3072, 5120], P('section', 'tensor'), may hold values from -6 to 6
- window: int32 [32], P('tensor'), may hold values from 96 to 192, as said below
- w_query: bfloat16 [5120, 4096], P(None, 'tensor'), may hold values from -0.078125 to 0.078125
- w_key: bfloat16 [5120, 4096], P(None, 'tensor'), may hold values from -0.078125 to 0.078125
- w_value: bfloat16 [5120, 4096], P(None, 'tensor'), may hold values from -0.078125 to 0.078125
- w_out: bfloat16 [4096, 5120], P('tensor'), may hold values from -0.09375 to 0.09375
Outputs:
- input_grad: bfloat16 [3072, 5120], P('section', 'tensor')
- query_weight_grad: float32 [5120, 4096], P('section', 'tensor')
- key_weight_grad: float32 [5120, 4096], P('section', 'tensor')
- value_weight_grad: float32 [5120, 4096], P('section', 'tensor')
- out_weight_grad: float32 [4096, 5120], P('tensor', 'section')
The draws below stay inside these ranges and needn't reach their ends.
Inputs may be any that keep to these rules, and one draw needn't show every extreme that they name: `window`: the number of most recent positions, the query's own included, that a head sees; some head has exactly 192.
All inputs are finite; a program needn't handle non-finite values.
Results may differ from the reference program's by a relative error of at most 0.025.
Values may be sent and summed in bfloat16 or wider, within the bound.
No kernel may reach another device: no remote copies, remote signals or barrier semaphores. Data moves between devices by JAX's collectives and lax.ppermute only.
A program may use at most 192 MiB of HBM per device.

```python
import math
import jax
import jax.numpy as jnp
from jax import lax

D = 5120
HEADS = 32
HD = 128
WMAX = 192
TOK_DEV = 384
TOKENS = 3072
N_SECTION = 8


def paired_rows(key):
    shape = (TOKENS, HEADS * HD)
    base_query = jnp.clip(jax.random.normal(jax.random.fold_in(key, 11), shape, jnp.float32), -4.6, 4.6)
    base_key = jnp.clip(jax.random.normal(jax.random.fold_in(key, 12), shape, jnp.float32), -4.6, 4.6)
    return (base_query, base_key)


def draw_query_rows(key, part):
    return paired_rows(key)[0].astype(jnp.bfloat16)


def draw_key_rows(key, part):
    return paired_rows(key)[1].astype(jnp.bfloat16)


def draw_window(key, part):
    lengths = jax.random.randint(jax.random.fold_in(key, 21), (HEADS,), WMAX // 2, WMAX + 1)
    chosen = jax.random.randint(jax.random.fold_in(key, 22), (), 0, HEADS)
    return jnp.where(jnp.arange(HEADS) == chosen, WMAX, lengths).astype(jnp.int32)


def steps_of(own_key, extent, shards, smallest, high):
    def one(position, shards_of):
        draws = jax.random.uniform(jax.random.fold_in(jax.random.fold_in(own_key, 6), position), (shards_of,), jnp.float32, smallest / len(shards), high / len(shards))
        return jnp.repeat(jnp.exp(draws), extent[position] // shards_of).reshape((-1,) + (1,) * (len(extent) - position - 1))

    loudness = one(*shards[0])
    for cut in shards[1:]:
        loudness = loudness * one(*cut)
    return loudness


def bell_draw(key, dims, width, reach, pieces=(), kind=jnp.bfloat16):
    values = width * jax.random.normal(key, dims, jnp.float32)
    if pieces:
        values = values * steps_of(key, dims, pieces, -0.22, 0.18)
    return jnp.clip(values, -reach, reach).astype(kind)


def setup_inputs(seed: int = 0) -> dict:
    splits = jax.random.split(jax.random.key(seed), 11)
    return {
        "layer_input": bell_draw(splits[0], (TOKENS, D), 1.0, 6.0, ((0, 8), (1, 4))),
        "query_rows": draw_query_rows(jax.random.fold_in(splits[10], 71), 0),
        "key_rows": draw_key_rows(jax.random.fold_in(splits[10], 71), 0),
        "value_rows": bell_draw(splits[3], (TOKENS, HEADS * HD), 1.0, 6.0, ((0, 8), (1, 4))),
        "out_grad": bell_draw(splits[4], (TOKENS, D), 1.0, 6.0, ((0, 8), (1, 4))),
        "window": draw_window(jax.random.fold_in(splits[10], 71), 0),
        "w_query": bell_draw(splits[6], (D, HEADS * HD), D ** -0.5, 0.078125, ((1, 4),)),
        "w_key": bell_draw(splits[7], (D, HEADS * HD), D ** -0.5, 0.078125, ((1, 4),)),
        "w_value": bell_draw(splits[8], (D, HEADS * HD), D ** -0.5, 0.078125, ((1, 4),)),
        "w_out": bell_draw(splits[9], (HEADS * HD, D), (HEADS * HD) ** -0.5, 0.09375, ((0, 4),)),
    }


def window_backward(query_rows, key_rows, value_rows, grad_rows, window, first_row):
    row_count = query_rows.shape[0]
    key_count = key_rows.shape[0]
    span = key_count - row_count
    head_count = query_rows.shape[1] // HD
    scaling = 1.0 / math.sqrt(HD)
    query_heads = query_rows.reshape(row_count, head_count, HD).astype(jnp.float32)
    key_heads = key_rows.reshape(key_count, head_count, HD).astype(jnp.float32)
    value_heads = value_rows.reshape(key_count, head_count, HD).astype(jnp.float32)
    grad_heads = grad_rows.reshape(row_count, head_count, HD).astype(jnp.float32)
    query_pos = first_row + jnp.arange(row_count, dtype=jnp.int32)
    key_pos = first_row - span + jnp.arange(key_count, dtype=jnp.int32)
    distance = query_pos[:, None] - key_pos[None, :]
    visible = (distance[None] >= 0) & (distance[None] < window[:, None, None]) & (key_pos[None, None, :] >= 0)
    scores = jnp.einsum('thd,khd->htk', query_heads, key_heads) * scaling
    scores = jnp.where(visible, scores, -jnp.inf)
    row_max = lax.optimization_barrier(jnp.max(scores, axis=2, keepdims=True))
    expon = jnp.exp(scores - row_max)
    probs = expon / lax.optimization_barrier(jnp.sum(expon, axis=2, keepdims=True))
    probs_low = probs.astype(jnp.bfloat16)
    attended = jnp.einsum('htk,khd->thd', probs_low.astype(jnp.float32), value_heads).astype(jnp.bfloat16)
    prob_grad = jnp.einsum('thd,khd->htk', grad_heads, value_heads)
    row_term = lax.optimization_barrier(jnp.sum(grad_heads * attended.astype(jnp.float32), axis=2))
    score_grad = (probs * (prob_grad - jnp.transpose(row_term)[:, :, None])).astype(jnp.bfloat16)
    score_wide = score_grad.astype(jnp.float32)
    grad_query = jnp.einsum('htk,khd->thd', score_wide, key_heads) * scaling
    grad_key = jnp.einsum('htk,thd->khd', score_wide, query_heads) * scaling
    grad_value = jnp.einsum('htk,thd->khd', probs_low.astype(jnp.float32), grad_heads)
    cols = head_count * HD
    return (attended.reshape(row_count, cols), grad_query.reshape(row_count, cols), grad_key.reshape(key_count, cols), grad_value.reshape(key_count, cols))

def reference(layer_input, query_rows, key_rows, value_rows, out_grad, window, w_query, w_key, w_value, w_out):
    cols = query_rows.shape[1]
    head_grad = jnp.dot(out_grad, w_out.T, preferred_element_type=jnp.float32).astype(jnp.bfloat16)
    padding = jnp.zeros((WMAX, cols), jnp.bfloat16)
    key_pad = jnp.concatenate([padding, key_rows], axis=0)
    value_pad = jnp.concatenate([padding, value_rows], axis=0)

    def one_block(block):
        start = (block * TOK_DEV).astype(jnp.int32)
        query_part = lax.dynamic_slice_in_dim(query_rows, start, TOK_DEV, 0)
        grad_part = lax.dynamic_slice_in_dim(head_grad, start, TOK_DEV, 0)
        key_part = lax.dynamic_slice_in_dim(key_pad, start, WMAX + TOK_DEV, 0)
        value_part = lax.dynamic_slice_in_dim(value_pad, start, WMAX + TOK_DEV, 0)
        return window_backward(query_part, key_part, value_part, grad_part, window, start)
    attended, grad_query, grad_key, grad_value = lax.map(one_block, jnp.arange(N_SECTION, dtype=jnp.int32))

    def carried(parts):
        later = jnp.concatenate([parts[1:, :WMAX], jnp.zeros((1, WMAX, cols), parts.dtype)], axis=0)
        own = parts[:, WMAX:]
        own = own.at[:, TOK_DEV - WMAX:].add(later)
        return own.reshape(TOKENS, cols).astype(jnp.bfloat16)
    attended = attended.reshape(TOKENS, cols)
    query_grad = grad_query.reshape(TOKENS, cols).astype(jnp.bfloat16)
    key_grad = carried(grad_key)
    value_grad = carried(grad_value)
    summed = jnp.dot(query_grad, w_query.T, preferred_element_type=jnp.float32)
    summed = summed + jnp.dot(key_grad, w_key.T, preferred_element_type=jnp.float32)
    summed = summed + jnp.dot(value_grad, w_value.T, preferred_element_type=jnp.float32)
    input_grad = summed.astype(jnp.bfloat16)
    query_weight_grad = jnp.dot(layer_input.T, query_grad, preferred_element_type=jnp.float32)
    key_weight_grad = jnp.dot(layer_input.T, key_grad, preferred_element_type=jnp.float32)
    value_weight_grad = jnp.dot(layer_input.T, value_grad, preferred_element_type=jnp.float32)
    out_weight_grad = jnp.dot(attended.T, out_grad, preferred_element_type=jnp.float32)
    return (input_grad, query_weight_grad, key_weight_grad, value_weight_grad, out_weight_grad)
```

```python
import math

import jax
import jax.numpy as jnp
from jax import lax
from jax.sharding import PartitionSpec as P

HD = 128
WMAX = 192


BY_COLS = (((1,), (1,)), ((), ()))
BY_ROWS = (((0,), (0,)), ((), ()))


def dot(a, b, dims):
    return lax.dot_general(a, b, dims, preferred_element_type=jnp.float32)


def swap(x, axis, mask):
    return lax.ppermute(x, axis, [(i, i ^ mask) for i in range(lax.axis_size(axis))])


def pick(x, index, axis=0):
    return lax.dynamic_index_in_dim(x, index, axis, keepdims=False)


def from_behind(x, axis, by):
    length = lax.axis_size(axis)
    pairs = [(i, i + by) for i in range(length) if 0 <= i + by < length]
    return lax.ppermute(x, axis, pairs)


def tensor_bits():
    count = lax.axis_size("tensor").bit_length() - 1
    index = lax.axis_index("tensor")
    return [(1 << b, (index >> b) & 1) for b in reversed(range(count))]


def tensor_gather(x):
    own = x.shape
    for place, (mask, bit) in enumerate(tensor_bits()):
        other = swap(x, "tensor", mask)
        first = jnp.where(bit == 0, x, other)
        second = jnp.where(bit == 0, other, x)
        x = jnp.stack([first, second], axis=place)
    return x.reshape((-1,) + own)


def tensor_exchange(x):
    own = x.shape
    bits = tensor_bits()
    x = x.reshape((2,) * len(bits) + own[1:])
    for mask, bit in bits:
        keep, send = pick(x, bit), pick(x, 1 - bit)
        other = swap(send, "tensor", mask)
        first = jnp.where(bit == 0, keep, other)
        second = jnp.where(bit == 0, other, keep)
        x = jnp.stack([first, second], axis=len(bits) - 1)
    return x.reshape(own)


def tensor_sum(x):
    rows = x.shape[0]
    bits = tensor_bits()[::-1]
    x = x.reshape((rows,) + (2,) * len(bits) + (-1,))
    for place, (mask, bit) in enumerate(bits):
        axis = len(bits) - place
        send = pick(x, 1 - bit, axis).astype(jnp.bfloat16)
        x = pick(x, bit, axis) + swap(send, "tensor", mask).astype(jnp.float32)
    return x


class Line:
    def __init__(self):
        size = lax.axis_size("section")
        self.long = math.gcd(size, 4)
        self.across = size // self.long
        self.z = lax.axis_index("section") // self.across
        self.x = lax.axis_index("section") % self.across
        self.middle = (self.z == 1) | (self.z == 2)

    def move(self, x, pairs):
        return lax.ppermute(
            x,
            "section",
            [(a * self.across + i, b * self.across + i) for a, b in pairs for i in range(self.across)],
        )

    def swap_z(self, x, mask):
        return self.move(x, [(i, i ^ mask) for i in range(self.long)])

    def ordered(self, near, far):
        return jnp.where(self.middle, far, near), jnp.where(self.middle, near, far)

    def gather(self, x):
        blocks = [x]
        if self.long > 1:
            blocks.append(self.swap_z(x, 1))
        if self.long == 4:
            for block in tuple(blocks):
                inner = self.move(block, [(1, 2), (2, 1)])
                outer = self.move(inner, [(1, 0), (2, 3)])
                blocks.append(jnp.where(self.middle, inner, outer))
        return jnp.concatenate(blocks, axis=0)

    def spread(self, x):
        count, few, width = x.shape
        x = x.reshape(self.long, count // self.long, few, width)
        parts = [self.swap_z(pick(x, self.z ^ k), k) if k else pick(x, self.z) for k in range(self.long)]
        if self.long == 4:
            parts[2:] = self.ordered(*parts[2:])
        x = tensor_gather(jnp.stack(parts))
        x = jnp.transpose(x, (1, 0, 3, 2, 4))
        return x.reshape(self.long * count * few, count // self.long * width)

    def tile(self, x, k):
        width = x.shape[1] // self.across
        return lax.dynamic_slice_in_dim(x, (self.x ^ k) * width, width, 1)

    def swap_x(self, x, k):
        size = self.across * self.long
        return lax.ppermute(x, "section", [(i, i ^ k) for i in range(size)])

    def summed(self, product):
        others = [self.swap_x(product(k).astype(jnp.bfloat16), k) for k in range(1, self.across)]
        total = product(0)
        for other in others:
            total = total + other.astype(jnp.float32)
        return total


def window_backward(query_rows, key_rows, value_rows, grad_rows, window, first_row):
    row_count = query_rows.shape[0]
    key_count = key_rows.shape[0]
    span = key_count - row_count
    head_count = query_rows.shape[1] // HD
    scaling = 1.0 / math.sqrt(HD)
    query_heads = query_rows.reshape(row_count, head_count, HD)
    key_heads = key_rows.reshape(key_count, head_count, HD)
    value_heads = value_rows.reshape(key_count, head_count, HD)
    grad_heads = grad_rows.reshape(row_count, head_count, HD)
    query_pos = first_row + jnp.arange(row_count, dtype=jnp.int32)
    key_pos = first_row - span + jnp.arange(key_count, dtype=jnp.int32)
    distance = query_pos[:, None] - key_pos[None, :]
    visible = (
        (distance[None] >= 0)
        & (distance[None] < window[:, None, None])
        & (key_pos[None, None, :] >= 0)
    )
    scores = (
        jnp.einsum("thd,khd->htk", query_heads, key_heads, preferred_element_type=jnp.float32)
        * scaling
    )
    scores = jnp.where(visible, scores, -jnp.inf)
    row_max = jnp.max(scores, axis=2, keepdims=True)
    expon = jnp.exp(scores - row_max)
    probs = expon / jnp.sum(expon, axis=2, keepdims=True)
    probs_low = probs.astype(jnp.bfloat16)
    attended = jnp.einsum(
        "htk,khd->thd", probs_low, value_heads, preferred_element_type=jnp.float32
    ).astype(jnp.bfloat16)
    prob_grad = jnp.einsum(
        "thd,khd->htk", grad_heads, value_heads, preferred_element_type=jnp.float32
    )
    row_term = jnp.sum(grad_heads.astype(jnp.float32) * attended.astype(jnp.float32), axis=2)
    score_grad = (probs * (prob_grad - jnp.transpose(row_term)[:, :, None])).astype(jnp.bfloat16)
    grad_query = (
        jnp.einsum("htk,khd->thd", score_grad, key_heads, preferred_element_type=jnp.float32)
        * scaling
    )
    grad_key = (
        jnp.einsum("htk,thd->khd", score_grad, query_heads, preferred_element_type=jnp.float32)
        * scaling
    )
    grad_value = jnp.einsum(
        "htk,thd->khd", probs_low, grad_heads, preferred_element_type=jnp.float32
    )
    cols = head_count * HD
    return (
        attended.reshape(row_count, cols),
        grad_query.reshape(row_count, cols),
        grad_key.reshape(key_count, cols),
        grad_value.reshape(key_count, cols),
    )


def local(
    layer_input, query_rows, key_rows, value_rows, out_grad, window, w_query, w_key, w_value, w_out
):
    line = Line()
    row_count, share = out_grad.shape
    count = lax.axis_size("tensor")
    few = row_count // count
    grad_parts = tensor_gather(out_grad)
    full_grad = jnp.transpose(grad_parts, (1, 0, 2)).reshape(row_count, count * share)
    head_grad = dot(full_grad, w_out, BY_COLS).astype(jnp.bfloat16)
    carried = from_behind(
        jnp.concatenate([key_rows[row_count - WMAX :], value_rows[row_count - WMAX :]], axis=0), "section", 1
    )
    first_row = lax.axis_index("section") * row_count
    attended, grad_query, key_all, value_all = window_backward(
        query_rows,
        jnp.concatenate([carried[:WMAX], key_rows], axis=0),
        jnp.concatenate([carried[WMAX:], value_rows], axis=0),
        head_grad,
        window,
        first_row,
    )
    back = from_behind(
        jnp.concatenate([key_all[:WMAX], value_all[:WMAX]], axis=0).astype(jnp.bfloat16), "section", -1
    ).astype(jnp.float32)
    query_grad = grad_query.astype(jnp.bfloat16)
    key_grad = key_all[WMAX:].at[row_count - WMAX :].add(back[:WMAX]).astype(jnp.bfloat16)
    value_grad = value_all[WMAX:].at[row_count - WMAX :].add(back[WMAX:]).astype(jnp.bfloat16)

    input_tile = line.spread(tensor_exchange(layer_input.reshape(count, few, share)))
    grad_tile = line.spread(
        lax.dynamic_slice_in_dim(grad_parts, lax.axis_index("tensor") * few, few, 1)
    )
    attended_line = line.gather(attended)
    out_weight_grad = line.summed(lambda k: dot(attended_line, line.tile(grad_tile, k), BY_ROWS))

    def weight_grad(grad):
        grad_line = line.gather(grad)
        return line.summed(lambda k: dot(line.tile(input_tile, k), grad_line, BY_ROWS))

    query_weight_grad = weight_grad(query_grad)
    key_weight_grad = weight_grad(key_grad)
    value_weight_grad = weight_grad(value_grad)
    partial_sum = dot(query_grad, w_query, BY_COLS)
    partial_sum = partial_sum + dot(key_grad, w_key, BY_COLS)
    partial_sum = partial_sum + dot(value_grad, w_value, BY_COLS)
    input_grad = tensor_sum(partial_sum).astype(jnp.bfloat16)
    return (input_grad, query_weight_grad, key_weight_grad, value_weight_grad, out_weight_grad)


def solution(mesh):
    in_specs = (
        P("section", "tensor"),
        P("section", "tensor"),
        P("section", "tensor"),
        P("section", "tensor"),
        P("section", "tensor"),
        P("tensor"),
        P(None, "tensor"),
        P(None, "tensor"),
        P(None, "tensor"),
        P("tensor", None),
    )
    out_specs = (
        P("section", "tensor"),
        P("section", "tensor"),
        P("section", "tensor"),
        P("section", "tensor"),
        P("tensor", "section"),
    )
    return jax.shard_map(local, mesh=mesh, in_specs=in_specs, out_specs=out_specs, check_vma=False)
```
